32 devices in a mesh: prow: 4 (over y, x), pcol: 8 (over z, core).
Axes of the slice: x: 2, y: 2, z: 4, core: 2. Of those that a mesh axis runs over, the one named last changes fastest.
Arguments:
- anc_inverse: bfloat16 [6, 1024, 3, 2048], P(None, 'prow', None, 'pcol'), may hold values from -0.078125 to 0.078125
- panel: bfloat16 [3, 6, 4, 256, 512], P(None, None, 'prow', 'pcol'), may hold values from -1.1953125 to 1.1953125
- tile_mask: int32 [3, 24], replicated, may hold values 0 or 1
- diag_inverse: float32 [3, 512, 512], P(None, ('prow', 'pcol')), may hold values from -6 to 6
Outputs:
- block_column: bfloat16 [3, 6, 4, 256, 512], P(None, None, 'prow', 'pcol')
- diag_block: float32 [3, 512, 512], P(None, ('prow', 'pcol'))
The draws below stay inside these ranges and needn't reach their ends.
All inputs are finite; a program needn't handle non-finite values.
Results may differ from the reference program's by a relative error of at most 0.0017.
Values may be sent and summed in bfloat16 or wider, within the bound.
No kernel may reach another device: no remote copies, remote signals or barrier semaphores. Data moves between devices by JAX's collectives and lax.ppermute only.
A program may use at most 128 MiB of HBM per device.

```python
import jax
import jax.numpy as jnp
from jax import lax

TILE = 256
W = 512
S = 3
CT = 3
TILES = 24
RT = 6
N_PROW = 4
N_PCOL = 8


def set_ends(entries, own_key, low, high):
    place = [jax.random.randint(jax.random.fold_in(own_key, axis), (), 0, length) for axis, length in enumerate(entries.shape)]
    main_axis = entries.shape.index(max(entries.shape))
    neighbour = place[:main_axis] + [(place[main_axis] + 1) % entries.shape[main_axis]] + place[main_axis + 1:]
    return entries.at[tuple(place)].set(low).at[tuple(neighbour)].set(high)


def steps_of(stream_key, extent, pieces, least, high):
    level = 1.0
    for position, shards_of in pieces:
        draws = jax.random.uniform(jax.random.fold_in(jax.random.fold_in(stream_key, 6), position), (shards_of,), jnp.float32, least / len(pieces), high / len(pieces))
        level = level * jnp.repeat(jnp.exp(draws), extent[position] // shards_of).reshape((-1,) + (1,) * (len(extent) - 1 - position))
    return level


def noise(own_key, extent, deviation, limit, pieces=(), held_as=jnp.bfloat16):
    loudness = steps_of(own_key, extent, pieces, -0.22, 0.18) if pieces else 1.0
    drawn = jax.random.normal(own_key, extent, jnp.float32) * deviation * loudness
    return jnp.minimum(jnp.maximum(drawn, -limit), limit).astype(held_as)


def setup_inputs(seed: int = 0) -> dict:
    splits = jax.random.split(jax.random.key(seed), 5)
    return {
        "anc_inverse": noise(splits[0], (RT, N_PROW * TILE, CT, N_PCOL * TILE), (TILES * TILE) ** -0.5, 0.078125, ((1, 4), (3, 8))),
        "panel": noise(splits[1], (S, RT, N_PROW, TILE, W), 0.15, 1.1953125, ((2, 4), (3, 8))),
        "tile_mask": set_ends((jax.random.randint(splits[2], (S, TILES), 0, 16) < 13).astype(jnp.int32), jax.random.fold_in(splits[2], 1), 0, 1),
        "diag_inverse": noise(splits[3], (S, W, W), 1.0, 6.0, ((1, 32),), jnp.float32),
    }


def reference(anc_inverse, panel, tile_mask, diag_inverse):
    order = anc_inverse.shape[0] * anc_inverse.shape[1]
    full = anc_inverse.reshape(order, order)
    panel_flat = panel.reshape(S, order, W)
    keeps = jnp.repeat(tile_mask, TILE, axis=1).astype(jnp.bfloat16)

    def single(items):
        lpanel, keep, dinv = items
        masked = lpanel * keep[:, None]
        product = jnp.dot(full, masked, preferred_element_type=jnp.float32)
        column = (-product * keep[:, None].astype(jnp.float32)).astype(jnp.bfloat16)
        diag = dinv - jnp.dot(masked.T, column, preferred_element_type=jnp.float32)
        return column, diag

    columns, diags = lax.map(single, (panel_flat, keeps, diag_inverse))
    return columns.reshape(panel.shape), diags
```

```python
import jax
import jax.numpy as jnp
from jax import lax
from jax.sharding import PartitionSpec as P

CORES = 2


def line(n_col, senders, step):
    return [
        (z * CORES + c, (z + step) * CORES + c) for z in senders for c in range(CORES)
    ]


def swap(x, n_col):
    return lax.ppermute(x, "pcol", [(q, q ^ 1) for q in range(n_col)])


def gather_rows(x, n_row):
    wide = jnp.broadcast_to(x[None], (n_row,) + x.shape)
    return lax.all_to_all(wide, "prow", 0, 0, tiled=True)


def spread_columns(masked, n_row, n_col):
    sets, tile_rows, sub, width = masked.shape
    tile_cols = tile_rows * n_row // n_col
    n_line = n_col // CORES
    piece = sub // n_row
    x = masked.reshape(sets, tile_rows, n_row, piece, width)
    x = lax.all_to_all(jnp.transpose(x, (2, 0, 1, 3, 4)), "prow", 0, 0, tiled=True)
    x = jnp.transpose(x, (2, 0, 1, 3, 4))
    x = x.reshape(tile_cols, n_line, CORES, sets, piece, CORES, width // CORES)
    x = jnp.transpose(x, (1, 5, 3, 0, 2, 4, 6))
    x = x.reshape((n_col,) + x.shape[2:])
    x = lax.all_to_all(x, "pcol", 0, 0, tiled=True)
    x = gather_rows(x, n_row)
    x = jnp.transpose(x, (2, 3, 4, 1, 0, 5, 6))
    return x.reshape(sets, tile_cols, CORES, n_col * sub, width // CORES)


def reduce_line(partial, place, n_col):
    n_line = n_col // CORES
    shard = lambda k: lax.dynamic_index_in_dim(
        partial, jnp.clip(k, 0, n_line - 1), axis=1, keepdims=False
    )
    up = down = None
    for t in range(1, n_line):
        to_up = shard(place + n_line - t)
        to_down = shard(place - n_line + t)
        if t > 1:
            to_up = to_up + up
            to_down = to_down + down
        up = lax.ppermute(to_up, "pcol", line(n_col, range(t), 1))
        down = lax.ppermute(to_down, "pcol", line(n_col, range(n_line - t, n_line), -1))
    total = shard(place)
    if n_line > 1:
        total = total + up + down
    return total


def reduce_diag(value, n_row, n_col):
    width, half = value.shape
    n_line = n_col // CORES
    x = lax.all_to_all(value.reshape(n_row, width // n_row, half), "prow", 0, 0, tiled=True)
    x = jnp.sum(x, axis=0)
    x = lax.all_to_all(x.reshape(n_col, -1, half), "pcol", 0, 0, tiled=True)
    x = jnp.sum(x.reshape(n_line, CORES, -1, half), axis=0)
    return jnp.transpose(x, (1, 0, 2)).reshape(-1, width)


def body(anc_inverse, panel, tile_mask, diag_inverse):
    n_row = lax.axis_size("prow")
    n_col = lax.axis_size("pcol")
    row_pos = lax.axis_index("prow")
    col_pos = lax.axis_index("pcol")
    place, core = col_pos // CORES, col_pos % CORES
    sets, tile_rows, single, sub, width = panel.shape
    tiles = tile_mask.shape[1]
    n_line = n_col // CORES
    half = width // CORES
    row_ids = jnp.arange(tile_rows, dtype=jnp.int32) * n_row + row_pos
    hits = (row_ids[:, None] == jnp.arange(tiles, dtype=jnp.int32)[None, :]).astype(jnp.int32)
    row_mask = jnp.sum(tile_mask[:, None, :] * hits[None], axis=2)
    keep = row_mask.astype(jnp.bfloat16)[:, :, None, None]
    masked = panel[:, :, 0] * keep
    other_anc = swap(anc_inverse, n_col)
    columns = spread_columns(masked, n_row, n_col)
    other_masked = swap(masked, n_col)
    mine = lax.dynamic_index_in_dim(columns, core, axis=2, keepdims=False)
    others = lax.dynamic_index_in_dim(columns, 1 - core, axis=2, keepdims=False)
    keep32 = keep.astype(jnp.float32)
    blocks, diags = [], []
    for s in range(sets):
        product = jnp.einsum(
            "aibj,bjw->aiw", anc_inverse, mine[s], preferred_element_type=jnp.float32
        ) + jnp.einsum(
            "aibj,bjw->aiw", other_anc, others[s], preferred_element_type=jnp.float32
        )
        partial = product.reshape(tile_rows, n_line, CORES * sub, half)
        total = reduce_line(partial, place, n_col)
        image = (-total * keep32[s]).astype(jnp.bfloat16)
        image = image.reshape(tile_rows, CORES, sub, half)
        stay = lax.dynamic_index_in_dim(image, core, axis=1, keepdims=False)
        leave = lax.dynamic_index_in_dim(image, 1 - core, axis=1, keepdims=False)
        came = swap(leave, n_col)
        low = jnp.where(core == 0, stay, came)
        high = jnp.where(core == 0, came, stay)
        blocks.append(jnp.concatenate([low, high], axis=-1))
        value = jnp.einsum(
            "axw,axv->wv", masked[s], stay, preferred_element_type=jnp.float32
        ) + jnp.einsum(
            "axw,axv->wv", other_masked[s], leave, preferred_element_type=jnp.float32
        )
        diags.append(reduce_diag(value, n_row, n_col))
    block_column = jnp.stack(blocks)[:, :, None]
    diag_block = diag_inverse - jnp.stack(diags)
    return (block_column, diag_block)


def solution(mesh):
    in_specs = (
        P(None, "prow", None, "pcol"),
        P(None, None, "prow", "pcol", None),
        P(),
        P(None, ("prow", "pcol"), None),
    )
    out_specs = (P(None, None, "prow", "pcol", None), P(None, ("prow", "pcol"), None))
    return jax.shard_map(body, mesh=mesh, in_specs=in_specs, out_specs=out_specs, check_vma=False)
```

```python
import functools

import jax
import jax.numpy as jnp
from jax import lax
from jax.experimental import pallas as pl
from jax.experimental.pallas import tpu as pltpu
from jax.sharding import PartitionSpec as P


CORES = 2
CHUNKS = 3


def by_col(x, n_col, k):
    return lax.ppermute(x, "pcol", [(q, q ^ k) for q in range(n_col)])


def by_row(x, n_row, k):
    return lax.ppermute(x, "prow", [(p, p ^ k) for p in range(n_row)])


def pick(x, index, axis):
    return lax.dynamic_index_in_dim(x, index, axis=axis, keepdims=False)


def product_kernel(counts, groups, pos, *refs):
    n_row = len(counts)
    refs, rest = refs[: sum(counts)], refs[sum(counts) :]
    blocks = []
    for count in counts:
        blocks.append(refs[:count])
        refs = refs[count:]
    pieces, outs, held = rest[:n_row], rest[n_row : n_row + groups], rest[n_row + groups]
    place, group, turn = pos[0], pos[1], pos[2]
    n_line, tile_cols, rows, _ = pieces[0].shape
    tile = n_line * rows
    for k in range(n_row):
        for j in range(n_line):
            start = pl.multiple_of((place ^ j) * rows, rows)
            for b in range(tile_cols):
                part = (k ^ turn) * tile_cols + b
                held[pl.ds(pl.multiple_of(part * tile, tile) + start, rows), :] = pieces[k][j, b]

    def left(block, b, r):
        parts = [x[:, b, group ^ r].reshape(x.shape[0] * rows, tile) for x in block]
        return parts[0] if len(parts) == 1 else jnp.concatenate(parts, axis=0)

    for r in reversed(range(groups)):
        wide = jnp.concatenate(
            [left(block, b, r) for block in blocks for b in range(tile_cols)], axis=1
        )
        outs[r][...] = jnp.dot(wide, held[...], preferred_element_type=jnp.float32)


def product(pos, blocks, pieces):
    n_row = len(blocks)
    _, tile_cols, groups, rows, tile = blocks[0][0].shape
    half = pieces[0].shape[-1]
    height = sum(x.shape[0] for x in blocks[0]) * rows
    depth = n_row * tile_cols * tile
    flat = [x for block in blocks for x in block]
    vmem = pl.BlockSpec(memory_space=pltpu.VMEM)
    return pl.pallas_call(
        functools.partial(product_kernel, tuple(len(block) for block in blocks), groups),
        out_shape=[jax.ShapeDtypeStruct((height, half), jnp.float32)] * groups,
        in_specs=[pl.BlockSpec(memory_space=pltpu.SMEM)] + [vmem] * (len(flat) + n_row),
        out_specs=[vmem] * groups,
        scratch_shapes=[pltpu.VMEM((depth, half), jnp.bfloat16)],
        cost_estimate=pl.CostEstimate(
            flops=2 * groups * height * depth * half,
            bytes_accessed=2 * depth * (groups * height + half) + 4 * groups * height * half,
            transcendentals=0,
        ),
    )(pos, *flat, *pieces)


def share_panel(x, group, groups, members, n_col):
    got = [pick(x, group, 1)]
    for k in range(1, groups):
        got.append(by_col(pick(x, group ^ k, 1), n_col, k * members * CORES))
    got = jnp.stack(got)
    all_got = [got] + [by_col(got, n_col, m * CORES) for m in range(1, members)]
    return jnp.stack(all_got, axis=1).reshape((-1,) + got.shape[1:])


def reduce_groups(parts, groups, members, n_col):
    k = 1
    while k < groups:
        parts = [
            parts[r] + by_col(parts[r + 1], n_col, k * members * CORES)
            for r in range(0, len(parts), 2)
        ]
        k *= 2
    return parts[0]


def reduce_diag(value, n_row, n_col):
    width, half = value.shape
    n_line = n_col // CORES
    x = lax.all_to_all(value.reshape(n_row, width // n_row, half), "prow", 0, 0, tiled=True)
    x = jnp.sum(x, axis=0)
    x = lax.all_to_all(x.reshape(n_col, -1, half), "pcol", 0, 0, tiled=True)
    x = jnp.sum(x.reshape(n_line, CORES, -1, half), axis=0)
    return jnp.transpose(x, (1, 0, 2)).reshape(-1, width)


def step(anc_inverse, panel, tile_mask, diag_inverse):
    n_row = lax.axis_size("prow")
    n_col = lax.axis_size("pcol")
    row_pos = lax.axis_index("prow")
    col_pos = lax.axis_index("pcol")
    place, core = col_pos // CORES, col_pos % CORES
    sets, tile_rows, _, sub, width = panel.shape
    tiles = tile_mask.shape[1]
    n_line = n_col // CORES
    members = n_row // CORES
    groups = n_line // members
    group, within = place // members, place % members
    half = width // CORES
    row_ids = jnp.arange(tile_rows, dtype=jnp.int32) * n_row + row_pos
    hits = (row_ids[:, None] == jnp.arange(tiles, dtype=jnp.int32)[None, :]).astype(jnp.int32)
    row_mask = jnp.sum(tile_mask[:, None, :] * hits[None], axis=2)
    keep = row_mask.astype(jnp.bfloat16)[:, :, None, None]
    keep32 = keep.astype(jnp.float32)
    masked = panel[:, :, 0] * keep
    tile_cols = tile_rows // groups
    anc = jnp.transpose(anc_inverse, (0, 2, 1, 3))
    anc = anc.reshape(tile_rows, tile_cols, groups, members, CORES * sub, -1)
    count = CHUNKS if tile_rows % CHUNKS == 0 else 1
    own = [pick(anc, within, 3)]
    blocks = [own, [by_col(own[0], n_col, 1)]]
    for m in range(1, members):
        there, across = [], []
        for x in jnp.split(pick(anc, within ^ m, 3), count):
            there.append(by_col(x, n_col, m * CORES))
            across.append(by_col(there[-1], n_col, 1))
        blocks += [there, across]
    other = by_col(masked, n_col, 1)
    both = jnp.concatenate(
        [jnp.where(core == 0, masked, other), jnp.where(core == 0, other, masked)], axis=2
    )
    narrow = lax.dynamic_slice_in_dim(both, core * half, half, axis=3)
    narrow = narrow.reshape(sets, tile_cols, groups, CORES * sub, half)
    pos = jnp.stack([place, group, row_pos ^ (col_pos % n_row)]).astype(jnp.int32)
    outs, diags = [], []
    for s in range(sets):
        piece = share_panel(narrow[s], group, groups, members, n_col)
        pieces = [piece] + [by_row(piece, n_row, k) for k in range(1, n_row)]
        parts = product(pos, blocks, pieces)
        total = reduce_groups(parts, groups, members, n_col)
        total = total.reshape(tile_rows, CORES, sub, half)
        image = (-total * keep32[s, :, None]).astype(jnp.bfloat16)
        stay, leave = pick(image, core, 1), pick(image, 1 - core, 1)
        came = by_col(leave, n_col, 1)
        outs.append(
            jnp.concatenate(
                [jnp.where(core == 0, stay, came), jnp.where(core == 0, came, stay)], axis=-1
            )
        )
        value = jnp.einsum(
            "axw,axv->wv", both[s], image.reshape(tile_rows, -1, half),
            preferred_element_type=jnp.float32,
        )
        diags.append(reduce_diag(value, n_row, n_col))
    block_column = jnp.stack(outs)[:, :, None]
    diag_block = diag_inverse - jnp.stack(diags)
    return (block_column, diag_block)


def solution(mesh):
    in_specs = (
        P(None, "prow", None, "pcol"),
        P(None, None, "prow", "pcol", None),
        P(),
        P(None, ("prow", "pcol"), None),
    )
    out_specs = (P(None, None, "prow", "pcol", None), P(None, ("prow", "pcol"), None))
    return jax.shard_map(step, mesh=mesh, in_specs=in_specs, out_specs=out_specs, check_vma=False)
```

```python
import functools

import jax
import jax.numpy as jnp
from jax import lax
from jax.experimental import pallas as pl
from jax.experimental.pallas import tpu as pltpu
from jax.sharding import PartitionSpec as P


CORES = 2


def by_col(x, n_col, k):
    return lax.ppermute(x, "pcol", [(q, q ^ k) for q in range(n_col)])


def by_row(x, n_row, k):
    return lax.ppermute(x, "prow", [(p, p ^ k) for p in range(n_row)])


def pick(x, index, axis):
    return lax.dynamic_index_in_dim(x, index, axis=axis, keepdims=False)


def product_kernel(n_row, count, pos, *refs):
    blocks = [refs[i * n_row : (i + 1) * n_row] for i in range(count)]
    pieces, refs = refs[count * n_row : (count + 1) * n_row], refs[(count + 1) * n_row :]
    outs, held = refs[:count], refs[count]
    place, turn = pos[0], pos[1]
    n_line, tile_cols, rows, _ = pieces[0].shape
    tile_rows = blocks[0][0].shape[0]
    tile = n_line * rows
    for k in range(n_row):
        for j in range(n_line):
            start = pl.multiple_of((place ^ j) * rows, rows)
            for b in range(tile_cols):
                base = pl.multiple_of(((k ^ turn) * tile_cols + b) * tile, tile)
                held[pl.ds(base + start, rows), :] = pieces[k][j, b]
    for out, wide in zip(outs, blocks):
        wide = jnp.concatenate(
            [
                block[:, b].reshape(tile_rows * rows, tile)
                for block in wide
                for b in range(tile_cols)
            ],
            axis=1,
        )
        out[...] = jnp.dot(wide, held[...], preferred_element_type=jnp.float32)


def product(pos, blocks, pieces):
    count, n_row = len(blocks), len(pieces)
    tile_rows, tile_cols, rows, tile = blocks[0][0].shape
    half = pieces[0].shape[-1]
    height, depth = tile_rows * rows, n_row * tile_cols * tile
    vmem = pl.BlockSpec(memory_space=pltpu.VMEM)
    return pl.pallas_call(
        functools.partial(product_kernel, n_row, count),
        out_shape=[jax.ShapeDtypeStruct((height, half), jnp.float32)] * count,
        in_specs=[pl.BlockSpec(memory_space=pltpu.SMEM)] + [vmem] * ((count + 1) * n_row),
        out_specs=[vmem] * count,
        scratch_shapes=[pltpu.VMEM((depth, half), jnp.bfloat16)],
        cost_estimate=pl.CostEstimate(
            flops=2 * count * height * depth * half,
            bytes_accessed=2 * depth * (count * height + half) + 4 * count * height * half,
            transcendentals=0,
        ),
    )(pos, *[x for block in blocks for x in block], *pieces)


def share_panel(x, group, groups, members, n_col):
    got = [pick(x, group, 1)]
    for k in range(1, groups):
        got.append(by_col(pick(x, group ^ k, 1), n_col, k * members * CORES))
    got = jnp.stack(got)
    all_got = [got] + [by_col(got, n_col, m * CORES) for m in range(1, members)]
    return jnp.stack(all_got, axis=1).reshape((-1,) + got.shape[1:])


def share_rows(piece, n_row):
    return [piece] + [by_row(piece, n_row, k) for k in range(1, n_row)]


def reduce_groups(parts, groups, members, n_col):
    k = 1
    while k < groups:
        parts = [
            parts[r] + by_col(parts[r + 1], n_col, k * members * CORES)
            for r in range(0, len(parts), 2)
        ]
        k *= 2
    return parts[0]


def spread_sum(x, place, count, move):
    total = pick(x, place, 1)
    for k in range(1, count):
        total = total + move(pick(x, place ^ k, 1), k)
    return total


def reduce_rows(value, row_pos, n_row):
    x = value.reshape(1, n_row, -1, value.shape[-1])
    return spread_sum(x, row_pos, n_row, lambda y, k: by_row(y, n_row, k))


def reduce_places(values, place, n_line, n_col):
    x = jnp.concatenate(values)
    x = x.reshape(x.shape[0], n_line, -1, x.shape[-1])
    return spread_sum(x, place, n_line, lambda y, k: by_col(y, n_col, k * CORES))


def step(anc_inverse, panel, tile_mask, diag_inverse):
    n_row = lax.axis_size("prow")
    n_col = lax.axis_size("pcol")
    row_pos = lax.axis_index("prow")
    col_pos = lax.axis_index("pcol")
    place, core = col_pos // CORES, col_pos % CORES
    sets, tile_rows, _, sub, width = panel.shape
    tiles = tile_mask.shape[1]
    n_line = n_col // CORES
    members = n_row // CORES
    groups = n_line // members
    group, within = place // members, place % members
    half = width // CORES
    row_ids = jnp.arange(tile_rows, dtype=jnp.int32) * n_row + row_pos
    hits = (row_ids[:, None] == jnp.arange(tiles, dtype=jnp.int32)[None, :]).astype(jnp.int32)
    row_mask = jnp.sum(tile_mask[:, None, :] * hits[None], axis=2)
    keep = row_mask.astype(jnp.bfloat16)[:, :, None, None]
    keep32 = keep.astype(jnp.float32)
    masked = panel[:, :, 0] * keep
    tile_cols = tile_rows // groups
    anc = jnp.transpose(anc_inverse, (0, 2, 1, 3))
    anc = anc.reshape(tile_rows, tile_cols, groups, members, CORES * sub, -1)
    def chosen(m, r):
        x = lax.dynamic_index_in_dim(anc, group ^ r, axis=2, keepdims=False)
        return lax.dynamic_index_in_dim(x, within ^ m, axis=2, keepdims=False)

    blocks = []
    for r in range(groups):
        kept = [chosen(m, r) for m in range(members)]
        kept = kept[:1] + [by_col(kept[m], n_col, m * CORES) for m in range(1, members)]
        wide = []
        for x in kept:
            wide += [x, by_col(x, n_col, 1)]
        blocks.append(wide)
    other = by_col(masked, n_col, 1)
    both = jnp.concatenate(
        [jnp.where(core == 0, masked, other), jnp.where(core == 0, other, masked)], axis=2
    )
    narrow = lax.dynamic_slice_in_dim(both, core * half, half, axis=3)
    narrow = narrow.reshape(sets, tile_cols, groups, CORES * sub, half)
    pos = jnp.stack([place, row_pos ^ (col_pos % n_row)]).astype(jnp.int32)
    outs, values, diags = [], [], []
    for s in range(sets):
        piece = share_panel(narrow[s], group, groups, members, n_col)
        pieces = share_rows(piece, n_row)
        if s:
            parts = product(pos, blocks, pieces)
        else:
            parts = product(pos, blocks[-1:], pieces)
            parts = product(pos, blocks[:-1], pieces) + parts
        total = reduce_groups(parts, groups, members, n_col)
        total = total.reshape(tile_rows, CORES, sub, half)
        image = (-total * keep32[s, :, None]).astype(jnp.bfloat16)
        stay, leave = pick(image, core, 1), pick(image, 1 - core, 1)
        came = by_col(leave, n_col, 1)
        outs.append(
            jnp.concatenate(
                [jnp.where(core == 0, stay, came), jnp.where(core == 0, came, stay)], axis=-1
            )
        )
        value = jnp.einsum(
            "axw,axv->wv", both[s], image.reshape(tile_rows, -1, half),
            preferred_element_type=jnp.float32,
        )
        values.append(reduce_rows(value, row_pos, n_row))
        if s in (sets - 2, sets - 1):
            diags.append(reduce_places(values, place, n_line, n_col))
            values = []
    x = jnp.concatenate(diags)
    x = x.reshape(sets, CORES, -1, half)
    stay, leave = pick(x, core, 1), pick(x, 1 - core, 1)
    came = by_col(leave, n_col, 1)
    diag = jnp.concatenate(
        [jnp.where(core == 0, stay, came), jnp.where(core == 0, came, stay)], axis=-1
    )
    block_column = jnp.stack(outs)[:, :, None]
    return (block_column, diag_inverse - diag)


def solution(mesh):
    in_specs = (
        P(None, "prow", None, "pcol"),
        P(None, None, "prow", "pcol", None),
        P(),
        P(None, ("prow", "pcol"), None),
    )
    out_specs = (P(None, None, "prow", "pcol", None), P(None, ("prow", "pcol"), None))
    return jax.shard_map(step, mesh=mesh, in_specs=in_specs, out_specs=out_specs, check_vma=False)
```

```python
import functools

import jax
import jax.numpy as jnp
from jax import lax
from jax.experimental import pallas as pl
from jax.experimental.pallas import tpu as pltpu
from jax.sharding import PartitionSpec as P


CORES = 2


def by_col(x, n_col, k):
    return lax.ppermute(x, "pcol", [(q, q ^ k) for q in range(n_col)])


def by_row(x, n_row, k):
    return lax.ppermute(x, "prow", [(p, p ^ k) for p in range(n_row)])


def pick(x, index, axis):
    return lax.dynamic_index_in_dim(x, index, axis=axis, keepdims=False)


def product_kernel(n_row, count, pos, *refs):
    blocks = [refs[i * n_row : (i + 1) * n_row] for i in range(count)]
    pieces, refs = refs[count * n_row : (count + 1) * n_row], refs[(count + 1) * n_row :]
    outs, held = refs[:count], refs[count]
    place, turn = pos[0], pos[1]
    n_line, tile_cols, rows, _ = pieces[0].shape
    tile_rows = blocks[0][0].shape[0]
    tile = n_line * rows
    for k in range(n_row):
        for j in range(n_line):
            start = pl.multiple_of((place ^ j) * rows, rows)
            for b in range(tile_cols):
                base = pl.multiple_of(((k ^ turn) * tile_cols + b) * tile, tile)
                held[pl.ds(base + start, rows), :] = pieces[k][j, b]
    for out, wide in zip(outs, blocks):
        wide = jnp.concatenate(
            [
                block[:, b].reshape(tile_rows * rows, tile)
                for block in wide
                for b in range(tile_cols)
            ],
            axis=1,
        )
        out[...] = jnp.dot(wide, held[...], preferred_element_type=jnp.float32)


def product(pos, blocks, pieces):
    count, n_row = len(blocks), len(pieces)
    tile_rows, tile_cols, rows, tile = blocks[0][0].shape
    half = pieces[0].shape[-1]
    height, depth = tile_rows * rows, n_row * tile_cols * tile
    vmem = pl.BlockSpec(memory_space=pltpu.VMEM)
    return pl.pallas_call(
        functools.partial(product_kernel, n_row, count),
        out_shape=[jax.ShapeDtypeStruct((height, half), jnp.float32)] * count,
        in_specs=[pl.BlockSpec(memory_space=pltpu.SMEM)] + [vmem] * ((count + 1) * n_row),
        out_specs=[vmem] * count,
        scratch_shapes=[pltpu.VMEM((depth, half), jnp.bfloat16)],
        compiler_params=pltpu.CompilerParams(vmem_limit_bytes=54 << 20),
        cost_estimate=pl.CostEstimate(
            flops=2 * count * height * depth * half,
            bytes_accessed=2 * depth * (count * height + half) + 4 * count * height * half,
            transcendentals=0,
        ),
    )(pos, *[x for block in blocks for x in block], *pieces)


def share_panel(x, group, groups, members, n_col):
    got = [pick(x, group, 1)]
    for k in range(1, groups):
        got.append(by_col(pick(x, group ^ k, 1), n_col, k * members * CORES))
    got = jnp.stack(got)
    all_got = [got] + [by_col(got, n_col, m * CORES) for m in range(1, members)]
    return jnp.stack(all_got, axis=1).reshape((-1,) + got.shape[1:])


def share_rows(piece, n_row):
    return [piece] + [by_row(piece, n_row, k) for k in range(1, n_row)]


def reduce_groups(parts, groups, members, n_col):
    k = 1
    while k < groups:
        parts = [
            parts[r] + by_col(parts[r + 1], n_col, k * members * CORES)
            for r in range(0, len(parts), 2)
        ]
        k *= 2
    return parts[0]


def spread_sum(x, place, count, move):
    total = pick(x, place, 1)
    for k in range(1, count):
        total = total + move(pick(x, place ^ k, 1), k)
    return total


def reduce_rows(value, row_pos, n_row):
    x = value.reshape(1, n_row, -1, value.shape[-1])
    return spread_sum(x, row_pos, n_row, lambda y, k: by_row(y, n_row, k))


def reduce_places(values, place, n_line, n_col):
    x = jnp.concatenate(values)
    x = x.reshape(x.shape[0], n_line, -1, x.shape[-1])
    return spread_sum(x, place, n_line, lambda y, k: by_col(y, n_col, k * CORES))


def step(anc_inverse, panel, tile_mask, diag_inverse):
    n_row = lax.axis_size("prow")
    n_col = lax.axis_size("pcol")
    row_pos = lax.axis_index("prow")
    col_pos = lax.axis_index("pcol")
    place, core = col_pos // CORES, col_pos % CORES
    sets, tile_rows, _, sub, width = panel.shape
    tiles = tile_mask.shape[1]
    n_line = n_col // CORES
    members = n_row // CORES
    groups = n_line // members
    group, within = place // members, place % members
    half = width // CORES
    row_ids = jnp.arange(tile_rows, dtype=jnp.int32) * n_row + row_pos
    hits = (row_ids[:, None] == jnp.arange(tiles, dtype=jnp.int32)[None, :]).astype(jnp.int32)
    row_mask = jnp.sum(tile_mask[:, None, :] * hits[None], axis=2)
    keep = row_mask.astype(jnp.bfloat16)[:, :, None, None]
    keep32 = keep.astype(jnp.float32)
    raw = panel[:, :, 0]
    tile_cols = tile_rows // groups
    anc = jnp.transpose(anc_inverse, (0, 2, 1, 3))
    anc = anc.reshape(tile_rows, tile_cols, groups, members, CORES * sub, -1)
    def chosen(m, r):
        x = lax.dynamic_index_in_dim(anc, group ^ r, axis=2, keepdims=False)
        return lax.dynamic_index_in_dim(x, within ^ m, axis=2, keepdims=False)

    blocks = []
    for r in range(groups):
        kept = [chosen(m, r) for m in range(members)]
        kept = kept[:1] + [by_col(kept[m], n_col, m * CORES) for m in range(1, members)]
        wide = []
        for x in kept:
            wide += [x, by_col(x, n_col, 1)]
        blocks.append(wide)
    other = by_col(raw, n_col, 1)
    both, narrow = [], []
    for s in range(sets):
        low = jnp.where(core == 0, raw[s], other[s]) * keep[s]
        high = jnp.where(core == 0, other[s], raw[s]) * keep[s]
        x = jnp.concatenate([low, high], axis=1)
        both.append((low, high))
        x = lax.dynamic_slice_in_dim(x, core * half, half, axis=2)
        narrow.append(x.reshape(tile_cols, groups, CORES * sub, half))
    pos = jnp.stack([place, row_pos ^ (col_pos % n_row)]).astype(jnp.int32)
    products = []
    for s in range(sets):
        piece = share_panel(narrow[s], group, groups, members, n_col)
        pieces = share_rows(piece, n_row)
        if s:
            parts = product(pos, blocks, pieces)
        else:
            parts = product(pos, blocks[-1:], pieces)
            parts = product(pos, blocks[:-1], pieces) + parts
        products.append(parts)
    both = lax.optimization_barrier((both, products[-2:][0]))[0]
    outs, values, diags = [], [], []
    for s in range(sets):
        total = reduce_groups(products[s], groups, members, n_col)
        total = total.reshape(tile_rows, CORES, sub, half)
        image = (-total * keep32[s, :, None]).astype(jnp.bfloat16)
        stay, leave = pick(image, core, 1), pick(image, 1 - core, 1)
        came = by_col(leave, n_col, 1)
        outs.append(
            jnp.concatenate(
                [jnp.where(core == 0, stay, came), jnp.where(core == 0, came, stay)], axis=-1
            )
        )
        value = jnp.einsum(
            "axw,axv->wv",
            jnp.concatenate(both[s], axis=1),
            image.reshape(tile_rows, -1, half),
            preferred_element_type=jnp.float32,
        )
        values.append(reduce_rows(value, row_pos, n_row))
        if s in (sets - 2, sets - 1):
            diags.append(reduce_places(values, place, n_line, n_col))
            values = []
    x = jnp.concatenate(diags)
    x = x.reshape(sets, CORES, -1, half)
    stay, leave = pick(x, core, 1), pick(x, 1 - core, 1)
    came = by_col(leave, n_col, 1)
    diag = jnp.concatenate(
        [jnp.where(core == 0, stay, came), jnp.where(core == 0, came, stay)], axis=-1
    )
    block_column = jnp.stack(outs)[:, :, None]
    return (block_column, diag_inverse - diag)


def solution(mesh):
    in_specs = (
        P(None, "prow", None, "pcol"),
        P(None, None, "prow", "pcol", None),
        P(),
        P(None, ("prow", "pcol"), None),
    )
    out_specs = (P(None, None, "prow", "pcol", None), P(None, ("prow", "pcol"), None))
    return jax.shard_map(step, mesh=mesh, in_specs=in_specs, out_specs=out_specs, check_vma=False)
```
